32 devices in a mesh: seq: 8 (over y, x, core), tp: 4 (over z).
Axes of the slice: x: 2, y: 2, z: 4, core: 2. Of those that a mesh axis runs over, the one named last changes fastest.
Arguments:
- hidden_in: bfloat16 [6144, 4096], P(('seq', 'tp')), may hold values from -26 to 26
- norm_gain: float32 [4096], replicated, may hold values from 0.1 to 1.9
- w_qkv: bfloat16 [3, 4096, 2048], P(None, None, 'tp'), may hold values from -1 to 1
- w_out: bfloat16 [2048, 4096], P('tp'), may hold values from -0.125 to 0.125
Outputs:
- datastore: bfloat16 [6144, 4096], P(('seq', 'tp'))
The draws below stay inside these ranges and needn't reach their ends.
All inputs are finite; a program needn't handle non-finite values.
Results may differ from the reference program's by a relative error of at most 0.006.
Values may be sent and summed in bfloat16 or wider, within the bound.
No kernel may reach another device: no remote copies, remote signals or barrier semaphores. Data moves between devices by JAX's collectives and lax.ppermute only.
A program may use at most 128 MiB of HBM per device.

```python
import math
import jax
import jax.numpy as jnp
from jax import lax

D = 4096
HEADS = 32
HD = 64
SPAN = 512
TOKENS = 6144
STRIPE = 24
N_SEQ = 8
N_TP = 4


def draw_hidden_in(key, part):
    key_one = jax.random.fold_in(jax.random.fold_in(key, 11), 0)
    result = jnp.clip(jax.random.normal(key_one, (TOKENS, D), jnp.float32), -6.0, 6.0)
    return result.astype(jnp.bfloat16)


def draw_w_qkv(key, part):
    key_one = jax.random.fold_in(jax.random.fold_in(key, 23), 0)
    scaling = jnp.array([0.3, 1.0, 1.0], jnp.float32)[:, None, None] / math.sqrt(D)
    result = jnp.clip(jax.random.normal(key_one, (3, D, HEADS * HD), jnp.float32), -6.0, 6.0) * scaling
    return result.astype(jnp.bfloat16)


def block_scale(key, extent, cuts, least, high):
    gain, own = 1.0, jax.random.fold_in(key, 6)
    for dim, shards_of in cuts:
        draws = jnp.exp(jax.random.uniform(jax.random.fold_in(own, dim), (shards_of,), jnp.float32, least / len(cuts), high / len(cuts)))
        gain = gain * jnp.repeat(draws, extent[dim] // shards_of).reshape([-1 if axis == dim else 1 for axis in range(len(extent))])
    return gain


def centred(rng, shape, width, most, shards=(), held_as=jnp.bfloat16):
    gain = block_scale(rng, shape, shards, -0.22, 0.18) if shards else 1.0
    values = jax.random.normal(rng, shape, jnp.float32) * width * gain
    return jnp.minimum(jnp.maximum(values, -most), most).astype(held_as)


def setup_inputs(seed: int = 0) -> dict:
    seeds = jax.random.split(jax.random.key(seed), 5)
    hidden_in = draw_hidden_in(jax.random.fold_in(seeds[4], 71), 0)
    norm_gain = jnp.clip(1.0 + 0.18 * jax.random.normal(seeds[1], (D,), jnp.float32), 0.1, 1.9)
    w_qkv = draw_w_qkv(jax.random.fold_in(seeds[4], 71), 0)
    w_out = centred(seeds[3], (HEADS * HD, D), (HEADS * HD) ** -0.5, 0.125, ((0, 4),))
    return {"hidden_in": hidden_in, "norm_gain": norm_gain, "w_qkv": w_qkv, "w_out": w_out}


epsilon = 1e-06

def reference(hidden_in, norm_gain, w_qkv, w_out):
    widened = hidden_in.astype(jnp.float32)
    mean_square = lax.optimization_barrier(jnp.mean(widened * widened, axis=1, keepdims=True))
    normed = (widened * lax.rsqrt(mean_square + epsilon) * norm_gain[None, :]).astype(jnp.bfloat16)
    queries = jnp.dot(normed, w_qkv[0], preferred_element_type=jnp.float32).astype(jnp.bfloat16)
    keys_all = jnp.dot(normed, w_qkv[1], preferred_element_type=jnp.float32).astype(jnp.bfloat16)
    values_all = jnp.dot(normed, w_qkv[2], preferred_element_type=jnp.float32).astype(jnp.bfloat16)
    half_len = SPAN // 2
    quarter = SPAN // 4
    pad_keys = jnp.pad(keys_all, ((quarter, quarter), (0, 0)))
    pad_values = jnp.pad(values_all, ((quarter, quarter), (0, 0)))
    block_count = TOKENS // half_len

    def one_block(number):
        start = (number * half_len).astype(jnp.int32)
        query_block = lax.dynamic_slice_in_dim(queries, start, half_len, 0).astype(jnp.float32).reshape(half_len, HEADS, HD)
        key_block = lax.dynamic_slice_in_dim(pad_keys, start, SPAN, 0).astype(jnp.float32).reshape(SPAN, HEADS, HD)
        value_block = lax.dynamic_slice_in_dim(pad_values, start, SPAN, 0).astype(jnp.float32).reshape(SPAN, HEADS, HD)
        scores = jnp.einsum('qhd,khd->hqk', query_block, key_block, precision=lax.Precision.HIGHEST)
        key_place = start - quarter + jnp.arange(SPAN, dtype=jnp.int32)
        key_valid = jnp.logical_and(key_place >= 0, key_place < TOKENS)
        scores = jnp.where(key_valid[None, None, :], scores, -1e+30)
        row_max = lax.optimization_barrier(jnp.max(scores, axis=-1, keepdims=True))
        powers = jnp.exp(scores - row_max)
        weights = (powers / lax.optimization_barrier(jnp.sum(powers, axis=-1, keepdims=True))).astype(jnp.bfloat16)
        context = jnp.einsum('hqk,khd->qhd', weights.astype(jnp.float32), value_block, precision=lax.Precision.HIGHEST)
        return context.astype(jnp.bfloat16).reshape(half_len, HEADS * HD)
    contexts = lax.map(one_block, jnp.arange(block_count, dtype=jnp.int32))
    context = contexts.reshape(TOKENS, HEADS * HD)
    new_state = (widened + jnp.dot(context, w_out, preferred_element_type=jnp.float32)).astype(jnp.bfloat16)
    grouped = new_state.reshape(N_SEQ, N_TP, N_SEQ, STRIPE, D)
    return jnp.transpose(grouped, (2, 1, 0, 3, 4)).reshape(TOKENS, D)
```

```python
import functools

import jax
import jax.numpy as jnp
from jax import lax
from jax.experimental import pallas as pl
from jax.experimental.pallas import tpu as pltpu
from jax.sharding import PartitionSpec as P

HD = 64
SPAN = 512
LANES = 128
CHUNKS = 2

epsilon = 1e-06

VMEM = pl.BlockSpec(memory_space=pltpu.VMEM)
SMEM = pl.BlockSpec(memory_space=pltpu.SMEM)


def norm_kernel(x_ref, gain_ref, out_ref):
    wide = x_ref[...].astype(jnp.float32)
    mean_square = jnp.mean(wide * wide, axis=1, keepdims=True)
    out_ref[...] = (wide * lax.rsqrt(mean_square + epsilon) * gain_ref[...]).astype(out_ref.dtype)


def rms_scale(rows_in, norm_gain, tile=32):
    rows, width = rows_in.shape
    return pl.pallas_call(
        norm_kernel,
        grid=(rows // tile,),
        in_specs=[
            pl.BlockSpec((tile, width), lambda i: (i, 0)),
            pl.BlockSpec((1, width), lambda i: (0, 0)),
        ],
        out_specs=pl.BlockSpec((tile, width), lambda i: (i, 0)),
        out_shape=jax.ShapeDtypeStruct(rows_in.shape, jnp.bfloat16),
        cost_estimate=pl.CostEstimate(
            flops=4 * rows * width, bytes_accessed=4 * rows * width, transcendentals=rows
        ),
        name="norm",
    )(rows_in, norm_gain.reshape(1, width))


def attend_pair(query, key, value, low_out, high_out):
    quarter = SPAN // 4
    lane = lax.broadcasted_iota(jnp.int32, (1, LANES), 1)
    first = lane < HD
    results = []
    for mine in (first, jnp.logical_not(first)):
        scores = lax.dot_general(
            jnp.where(mine, query, jnp.zeros_like(query)),
            key,
            (((1,), (1,)), ((), ())),
            preferred_element_type=jnp.float32,
        )
        if low_out is not None:
            edge = jnp.where(low_out, -1e30, scores[:, :quarter])
            scores = jnp.concatenate([edge, scores[:, quarter:]], axis=1)
        if high_out is not None:
            edge = jnp.where(high_out, -1e30, scores[:, -quarter:])
            scores = jnp.concatenate([scores[:, :-quarter], edge], axis=1)
        row_max = jnp.max(scores, axis=-1, keepdims=True)
        powers = jnp.exp(scores - row_max).astype(jnp.bfloat16)
        padded = jnp.where(mine, value, jnp.ones_like(value))
        results.append(jnp.dot(powers, padded, preferred_element_type=jnp.float32))
    context = jnp.where(first, results[0], results[1])
    sums = jnp.where(first, results[1], results[0])
    sums = pltpu.roll(sums, HD, 1)
    return (context / sums).astype(jnp.bfloat16)


def inner_kernel(numbers, q_ref, k_ref, v_ref, out_ref):
    half_len, quarter = SPAN // 2, SPAN // 4

    @pl.loop(0, q_ref.shape[1] // LANES)
    def _(pair):
        lanes = pl.ds(pl.multiple_of(pair * LANES, LANES), LANES)
        for place, number in enumerate(numbers):
            start = number * half_len
            keys = slice(start - quarter, start - quarter + SPAN)
            out_ref[place * half_len : (place + 1) * half_len, lanes] = attend_pair(
                q_ref[start : start + half_len, lanes], k_ref[keys, lanes], v_ref[keys, lanes], None, None
            )


def outer_kernel(
    edge_ref, q_ref, k_ref, v_ref, low_k_ref, low_v_ref, high_k_ref, high_v_ref, first_ref, last_ref
):
    half_len, quarter = SPAN // 2, SPAN // 4
    rows = q_ref.shape[0]

    @pl.loop(0, q_ref.shape[1] // LANES)
    def _(pair):
        lanes = pl.ds(pl.multiple_of(pair * LANES, LANES), LANES)
        key = jnp.concatenate([low_k_ref[:, lanes], k_ref[: SPAN - quarter, lanes]], axis=0)
        value = jnp.concatenate([low_v_ref[:, lanes], v_ref[: SPAN - quarter, lanes]], axis=0)
        first_ref[:, lanes] = attend_pair(q_ref[:half_len, lanes], key, value, edge_ref[0] != 0, None)
        key = jnp.concatenate([k_ref[rows - SPAN + quarter :, lanes], high_k_ref[:, lanes]], axis=0)
        value = jnp.concatenate([v_ref[rows - SPAN + quarter :, lanes], high_v_ref[:, lanes]], axis=0)
        last_ref[:, lanes] = attend_pair(q_ref[rows - half_len :, lanes], key, value, None, edge_ref[1] != 0)


def attention_cost(blocks, width):
    half_len = SPAN // 2
    return pl.CostEstimate(
        flops=4 * blocks * half_len * SPAN * width,
        bytes_accessed=2 * blocks * (2 * half_len + 2 * SPAN) * width,
        transcendentals=blocks * half_len * SPAN * width // HD,
    )


def attend(queries, keys, values, low, high, at_start, at_end):
    half_len = SPAN // 2
    rows, width = queries.shape
    count = rows // half_len
    numbers = tuple(range(1, count - 1))
    inner = pl.pallas_call(
        functools.partial(inner_kernel, numbers),
        in_specs=[VMEM] * 3,
        out_specs=VMEM,
        out_shape=jax.ShapeDtypeStruct((len(numbers) * half_len, width), jnp.bfloat16),
        cost_estimate=attention_cost(len(numbers), width),
        name="inner_blocks",
    )(queries, keys, values)
    edges = jnp.stack([at_start, at_end]).astype(jnp.int32)
    first, last = pl.pallas_call(
        outer_kernel,
        in_specs=[SMEM] + [VMEM] * 7,
        out_specs=[VMEM] * 2,
        out_shape=[jax.ShapeDtypeStruct((half_len, width), jnp.bfloat16)] * 2,
        cost_estimate=attention_cost(2, width),
        name="outer_blocks",
    )(edges, queries, keys, values, *low, *high)
    return jnp.concatenate([first, inner, last], axis=0)


def project_kernel(context_ref, hidden_ref, w_ref, out_ref):
    product = jnp.dot(context_ref[...], w_ref[0], preferred_element_type=jnp.float32)
    out_ref[...] = (hidden_ref[...].astype(jnp.float32) + product).astype(out_ref.dtype)


def project(context, hidden, weights):
    rows, depth = context.shape
    count, _, columns = weights.shape
    return pl.pallas_call(
        project_kernel,
        grid=(count,),
        in_specs=[
            pl.BlockSpec((rows, depth), lambda i: (0, 0)),
            pl.BlockSpec((rows, columns), lambda i: (0, i)),
            pl.BlockSpec((1, depth, columns), lambda i: (i, 0, 0)),
        ],
        out_specs=pl.BlockSpec((rows, columns), lambda i: (0, i)),
        out_shape=jax.ShapeDtypeStruct(hidden.shape, jnp.bfloat16),
        cost_estimate=pl.CostEstimate(
            flops=2 * rows * depth * columns * count,
            bytes_accessed=2 * depth * columns * count,
            transcendentals=0,
        ),
        name="project",
    )(context, hidden, weights)


def on_device(hidden_in, norm_gain, w_qkv, w_out):
    seq_count, tp_count = lax.axis_size("seq"), lax.axis_size("tp")
    seq_index, tp_index = lax.axis_index("seq"), lax.axis_index("tp")
    own_rows, model_width = hidden_in.shape
    width = w_qkv.shape[2]
    quarter = SPAN // 4
    stripe = own_rows // seq_count
    rows = own_rows * tp_count
    columns = model_width // seq_count

    own_columns = lax.dynamic_slice_in_dim(w_out, seq_index * columns, columns, 1)
    gathered = lax.all_gather(own_columns, ("seq", "tp"), axis=0)
    gathered = gathered.reshape(seq_count, tp_count * width, columns)

    normed = rms_scale(hidden_in, norm_gain)
    chunk = own_rows // CHUNKS
    pieces = [normed[i * chunk : (i + 1) * chunk] for i in range(CHUNKS)]
    ring = [(i, (i + 1) % tp_count) for i in range(tp_count)]
    results = [jnp.zeros((rows, width), jnp.bfloat16) for _ in range(3)]
    hidden = None
    for step in range(tp_count):
        following = [lax.ppermute(piece, "tp", ring) for piece in pieces] if step < tp_count - 1 else None
        shard = lax.rem(tp_index - step + tp_count, tp_count)
        for i, piece in enumerate(pieces):
            for which in range(3):
                product = jnp.dot(piece, w_qkv[which], preferred_element_type=jnp.float32).astype(jnp.bfloat16)
                results[which] = lax.dynamic_update_slice(
                    results[which], product, (shard * own_rows + i * chunk, jnp.int32(0))
                )
        pieces = following
        if step == 0:
            hidden = lax.all_to_all(
                hidden_in.reshape(seq_count, stripe, model_width), "seq", split_axis=0, concat_axis=0, tiled=True
            ).reshape(own_rows, model_width)
        if step == 1:
            hidden, pieces = lax.optimization_barrier((hidden, pieces))
    queries, keys, values = results

    forward = [(i, i + 1) for i in range(seq_count - 1)]
    backward = [(i + 1, i) for i in range(seq_count - 1)]
    low = [lax.ppermute(a[rows - quarter :], "seq", forward) for a in (keys, values)]
    high = [lax.ppermute(a[:quarter], "seq", backward) for a in (keys, values)]
    context = attend(queries, keys, values, low, high, seq_index == 0, seq_index == seq_count - 1)

    sent = context.reshape(tp_count, seq_count, stripe, width).transpose(1, 0, 2, 3)
    sent = sent.reshape(seq_count * tp_count, stripe, width)
    got = lax.all_to_all(sent, ("seq", "tp"), split_axis=0, concat_axis=0, tiled=True)
    got = got.reshape(seq_count, tp_count, stripe, width).transpose(0, 2, 1, 3)
    return project(got.reshape(own_rows, tp_count * width), hidden, gathered)


def solution(mesh):
    return jax.shard_map(
        on_device,
        mesh=mesh,
        in_specs=(P(("seq", "tp"), None), P(), P(None, None, "tp"), P("tp", None)),
        out_specs=P(("seq", "tp"), None),
        check_vma=False,
    )
```

```python
import functools

import jax
import jax.numpy as jnp
from jax import lax
from jax.experimental import pallas as pl
from jax.experimental.pallas import tpu as pltpu
from jax.sharding import PartitionSpec as P

HD = 64
SPAN = 512
LANES = 128
CHUNKS = 2

epsilon = 1e-06

VMEM = pl.BlockSpec(memory_space=pltpu.VMEM)
SMEM = pl.BlockSpec(memory_space=pltpu.SMEM)


def norm_kernel(x_ref, gain_ref, out_ref):
    wide = x_ref[...].astype(jnp.float32)
    mean_square = jnp.mean(wide * wide, axis=1, keepdims=True)
    out_ref[...] = (wide * lax.rsqrt(mean_square + epsilon) * gain_ref[...]).astype(out_ref.dtype)


def rms_scale(rows_in, norm_gain, start, rows, tile=32):
    width = rows_in.shape[1]
    first = start // tile
    return pl.pallas_call(
        norm_kernel,
        grid=(rows // tile,),
        in_specs=[
            pl.BlockSpec((tile, width), lambda i: (i + first, 0)),
            pl.BlockSpec((1, width), lambda i: (0, 0)),
        ],
        out_specs=pl.BlockSpec((tile, width), lambda i: (i, 0)),
        out_shape=jax.ShapeDtypeStruct((rows, width), jnp.bfloat16),
        cost_estimate=pl.CostEstimate(
            flops=4 * rows * width, bytes_accessed=4 * rows * width, transcendentals=rows
        ),
        name="norm",
    )(rows_in, norm_gain.reshape(1, width))


def attend_pair(query, key, value, low_out, high_out):
    quarter = SPAN // 4
    lane = lax.broadcasted_iota(jnp.int32, (1, LANES), 1)
    first = lane < HD
    results = []
    for mine in (first, jnp.logical_not(first)):
        scores = lax.dot_general(
            jnp.where(mine, query, jnp.zeros_like(query)),
            key,
            (((1,), (1,)), ((), ())),
            preferred_element_type=jnp.float32,
        )
        if low_out is not None:
            edge = jnp.where(low_out, -1e30, scores[:, :quarter])
            scores = jnp.concatenate([edge, scores[:, quarter:]], axis=1)
        if high_out is not None:
            edge = jnp.where(high_out, -1e30, scores[:, -quarter:])
            scores = jnp.concatenate([scores[:, :-quarter], edge], axis=1)
        row_max = jnp.max(scores, axis=-1, keepdims=True)
        powers = jnp.exp(scores - row_max).astype(jnp.bfloat16)
        padded = jnp.where(mine, value, jnp.ones_like(value))
        results.append(jnp.dot(powers, padded, preferred_element_type=jnp.float32))
    context = jnp.where(first, results[0], results[1])
    sums = jnp.where(first, results[1], results[0])
    sums = pltpu.roll(sums, HD, 1)
    return (context / sums).astype(jnp.bfloat16)


def inner_kernel(numbers, q_ref, kv_ref, out_ref):
    half_len, quarter = SPAN // 2, SPAN // 4
    width = q_ref.shape[1]

    @pl.loop(0, width // LANES)
    def _(pair):
        lanes = pl.ds(pl.multiple_of(pair * LANES, LANES), LANES)
        v_lanes = pl.ds(pl.multiple_of(pair * LANES + width, LANES), LANES)
        for place, number in enumerate(numbers):
            start = number * half_len
            keys = slice(start - quarter, start - quarter + SPAN)
            out_ref[place * half_len : (place + 1) * half_len, lanes] = attend_pair(
                q_ref[start : start + half_len, lanes], kv_ref[keys, lanes], kv_ref[keys, v_lanes], None, None
            )


def outer_kernel(edge_ref, q_ref, kv_ref, low_ref, high_ref, first_ref, last_ref):
    half_len, quarter = SPAN // 2, SPAN // 4
    rows, width = q_ref.shape
    inside = SPAN - quarter

    @pl.loop(0, width // LANES)
    def _(pair):
        lanes = pl.ds(pl.multiple_of(pair * LANES, LANES), LANES)
        v_lanes = pl.ds(pl.multiple_of(pair * LANES + width, LANES), LANES)
        key = jnp.concatenate([low_ref[:, lanes], kv_ref[:inside, lanes]], axis=0)
        value = jnp.concatenate([low_ref[:, v_lanes], kv_ref[:inside, v_lanes]], axis=0)
        first_ref[:, lanes] = attend_pair(q_ref[:half_len, lanes], key, value, edge_ref[0] != 0, None)
        key = jnp.concatenate([kv_ref[rows - inside :, lanes], high_ref[:, lanes]], axis=0)
        value = jnp.concatenate([kv_ref[rows - inside :, v_lanes], high_ref[:, v_lanes]], axis=0)
        last_ref[:, lanes] = attend_pair(q_ref[rows - half_len :, lanes], key, value, None, edge_ref[1] != 0)


def attention_cost(blocks, width):
    half_len = SPAN // 2
    return pl.CostEstimate(
        flops=8 * blocks * half_len * SPAN * width,
        bytes_accessed=2 * blocks * (2 * half_len + 2 * SPAN) * width,
        transcendentals=blocks * half_len * SPAN * width // HD,
    )


def attend(queries, both, low, high, at_start, at_end):
    half_len = SPAN // 2
    rows, width = queries.shape
    count = rows // half_len
    numbers = tuple(range(1, count - 1))
    inner = pl.pallas_call(
        functools.partial(inner_kernel, numbers),
        in_specs=[VMEM] * 2,
        out_specs=VMEM,
        out_shape=jax.ShapeDtypeStruct((len(numbers) * half_len, width), jnp.bfloat16),
        cost_estimate=attention_cost(len(numbers), width),
        name="inner_blocks",
    )(queries, both)
    edges = jnp.stack([at_start, at_end]).astype(jnp.int32)
    first, last = pl.pallas_call(
        outer_kernel,
        in_specs=[SMEM] + [VMEM] * 4,
        out_specs=[VMEM] * 2,
        out_shape=[jax.ShapeDtypeStruct((half_len, width), jnp.bfloat16)] * 2,
        cost_estimate=attention_cost(2, width),
        name="outer_blocks",
    )(edges, queries, both, low, high)
    return jnp.concatenate([first, inner, last], axis=0)


def project_kernel(place_ref, entry_ref, order_ref, context_ref, hidden_ref, own_ref, *refs):
    parts, out_ref = refs[:-1], refs[-1]
    depth, part_depth = own_ref.shape[0], parts[0].shape[1]

    def columns(k, start, size):
        return context_ref[:, pl.ds(pl.multiple_of(order_ref[k] * depth + start, LANES), size)]

    total = hidden_ref[...].astype(jnp.float32)
    total += jnp.dot(columns(0, 0, depth), own_ref[...], preferred_element_type=jnp.float32)
    for i, part in enumerate(parts):
        k, h = divmod(i, 2)
        mine = columns(k + 1, h * part_depth, part_depth)
        total += jnp.dot(mine, part[0], preferred_element_type=jnp.float32)
    out_ref[...] = total.astype(out_ref.dtype)


def project(places, entries, order, context, hidden, own, shared):
    rows, width = hidden.shape
    count, part_depth, columns = shared[0][0].shape
    depth = own.shape[0]
    at = lambda e, places, entries, order: (0, places[e])
    holds = [
        lambda e, places, entries, order: (e, 0, 0),
        lambda e, places, entries, order: (entries[e], 0, 0),
    ]
    return pl.pallas_call(
        project_kernel,
        grid_spec=pltpu.PrefetchScalarGridSpec(
            num_scalar_prefetch=3,
            grid=(count,),
            in_specs=[
                pl.BlockSpec(context.shape, lambda e, places, entries, order: (0, 0)),
                pl.BlockSpec((rows, columns), at),
                pl.BlockSpec((depth, columns), at),
            ]
            + [pl.BlockSpec((1, part_depth, columns), holds[h]) for _ in shared for h in range(2)],
            out_specs=pl.BlockSpec((rows, columns), at),
        ),
        out_shape=jax.ShapeDtypeStruct(hidden.shape, jnp.bfloat16),
        cost_estimate=pl.CostEstimate(
            flops=2 * rows * context.shape[1] * width,
            bytes_accessed=2 * context.shape[1] * width,
            transcendentals=0,
        ),
        name="project",
    )(places, entries, order, context, hidden, own, *[a for pair in shared for a in pair])


def share_orders(seq_count):
    bits = [1 << i for i in range(seq_count.bit_length() - 1)]
    outer = bits[1:]
    return [outer + bits[:1], outer[::-1] + bits[:1]]


def share(piece, order, seq_count):
    held = piece[None]
    for bit in order:
        pairs = [(i, i ^ bit) for i in range(seq_count)]
        held = jnp.concatenate([held, lax.ppermute(held, "seq", pairs)], axis=0)
    return held


def offsets(order):
    held = [0]
    for bit in order:
        held = held + [offset ^ bit for offset in held]
    return held


def on_device(hidden_in, norm_gain, w_qkv, w_out):
    seq_count, tp_count = lax.axis_size("seq"), lax.axis_size("tp")
    seq_index, tp_index = lax.axis_index("seq"), lax.axis_index("tp")
    own_rows, model_width = hidden_in.shape
    width = w_qkv.shape[2]
    quarter = SPAN // 4
    stripe = own_rows // seq_count
    rows = own_rows * tp_count
    columns = model_width // seq_count
    ring = [(i, (i + 1) % tp_count) for i in range(tp_count)]

    weights = lax.dynamic_slice_in_dim(w_out, seq_index * columns, columns, 1)
    orders = share_orders(seq_count)
    shared = []

    chunk = own_rows // CHUNKS
    pieces = [rms_scale(hidden_in, norm_gain, i * chunk, chunk) for i in range(CHUNKS)]
    queries = jnp.zeros((rows, width), jnp.bfloat16)
    both = jnp.zeros((rows, 2 * width), jnp.bfloat16)
    hidden = None
    for step in range(tp_count):
        last = step == tp_count - 1
        following = None if last else [lax.ppermute(piece, "tp", ring) for piece in pieces]
        if not last:
            weights = lax.ppermute(weights, "tp", ring)
            shared.append(
                [
                    share(weights[h * width // 2 : (h + 1) * width // 2], orders[h], seq_count)
                    for h in range(2)
                ]
            )
        start = lax.rem(tp_index - step + tp_count, tp_count) * own_rows
        for i, piece in enumerate(pieces):
            products = [
                jnp.dot(piece, w_qkv[which], preferred_element_type=jnp.float32).astype(jnp.bfloat16)
                for which in range(3)
            ]
            at = start + i * chunk
            queries = lax.dynamic_update_slice(queries, products[0], (at, jnp.int32(0)))
            both = lax.dynamic_update_slice(both, products[1], (at, jnp.int32(0)))
            both = lax.dynamic_update_slice(both, products[2], (at, jnp.int32(width)))
        pieces = following
        if step == 0:
            hidden = lax.all_to_all(
                hidden_in.reshape(seq_count, stripe, model_width), "seq", split_axis=0, concat_axis=0, tiled=True
            ).reshape(own_rows, model_width)
        if step == 1:
            hidden, pieces = lax.optimization_barrier((hidden, pieces))

    forward = [(i, i + 1) for i in range(seq_count - 1)]
    backward = [(i + 1, i) for i in range(seq_count - 1)]
    low = lax.ppermute(both[rows - quarter :], "seq", forward)
    high = lax.ppermute(both[:quarter], "seq", backward)
    context = attend(queries, both, low, high, seq_index == 0, seq_index == seq_count - 1)

    sent = context.reshape(tp_count, seq_count, stripe, width).transpose(1, 0, 2, 3)
    sent = sent.reshape(seq_count * tp_count, stripe, width)
    got = lax.all_to_all(sent, ("seq", "tp"), split_axis=0, concat_axis=0, tiled=True)
    got = got.reshape(seq_count, tp_count, stripe, width).transpose(0, 2, 1, 3)
    first, second = [offsets(order) for order in orders]
    places = seq_index ^ jnp.array(first, jnp.int32)
    entries = jnp.array([second.index(offset) for offset in first], jnp.int32)
    order = lax.rem(tp_index - jnp.arange(tp_count, dtype=jnp.int32) + tp_count, tp_count)
    return project(places, entries, order, got.reshape(own_rows, tp_count * width), hidden, w_out, shared)


def solution(mesh):
    return jax.shard_map(
        on_device,
        mesh=mesh,
        in_specs=(P(("seq", "tp"), None), P(), P(None, None, "tp"), P("tp", None)),
        out_specs=P(("seq", "tp"), None),
        check_vma=False,
    )
```

```python
import functools

import jax
import jax.numpy as jnp
from jax import lax
from jax.experimental import pallas as pl
from jax.experimental.pallas import tpu as pltpu
from jax.sharding import PartitionSpec as P


HD = 64
SPAN = 512
LANES = 128
CHUNKS = 2
EARLY = 1
GRANT = 12 << 20

epsilon = 1e-06

VMEM = pl.BlockSpec(memory_space=pltpu.VMEM)
ANY = pl.BlockSpec(memory_space=pl.ANY)
SMEM = pl.BlockSpec(memory_space=pltpu.SMEM)


def norm_kernel(x_ref, gain_ref, out_ref):
    wide = x_ref[...].astype(jnp.float32)
    mean_square = jnp.mean(wide * wide, axis=1, keepdims=True)
    out_ref[...] = (wide * lax.rsqrt(mean_square + epsilon) * gain_ref[...]).astype(out_ref.dtype)


def rms_scale(rows_in, norm_gain, start, rows, tile=32):
    width = rows_in.shape[1]
    first = start // tile
    return pl.pallas_call(
        norm_kernel,
        grid=(rows // tile,),
        in_specs=[
            pl.BlockSpec((tile, width), lambda i: (i + first, 0)),
            pl.BlockSpec((1, width), lambda i: (0, 0)),
        ],
        out_specs=pl.BlockSpec((tile, width), lambda i: (i, 0)),
        out_shape=jax.ShapeDtypeStruct((rows, width), jnp.bfloat16),
        cost_estimate=pl.CostEstimate(
            flops=4 * rows * width, bytes_accessed=4 * rows * width, transcendentals=rows
        ),
        name="norm",
    )(rows_in, norm_gain.reshape(1, width))


def attend_pair(query, key, value, low_out, high_out):
    quarter = SPAN // 4
    lane = lax.broadcasted_iota(jnp.int32, (1, LANES), 1)
    first = lane < HD
    results = []
    for mine in (first, jnp.logical_not(first)):
        scores = lax.dot_general(
            jnp.where(mine, query, jnp.zeros_like(query)),
            key,
            (((1,), (1,)), ((), ())),
            preferred_element_type=jnp.float32,
        )
        if low_out is not None:
            edge = jnp.where(low_out, -1e30, scores[:, :quarter])
            scores = jnp.concatenate([edge, scores[:, quarter:]], axis=1)
        if high_out is not None:
            edge = jnp.where(high_out, -1e30, scores[:, -quarter:])
            scores = jnp.concatenate([scores[:, :-quarter], edge], axis=1)
        row_max = jnp.max(scores, axis=-1, keepdims=True)
        powers = jnp.exp(scores - row_max).astype(jnp.bfloat16)
        padded = jnp.where(mine, value, jnp.ones_like(value))
        results.append(jnp.dot(powers, padded, preferred_element_type=jnp.float32))
    context = jnp.where(first, results[0], results[1])
    sums = jnp.where(first, results[1], results[0])
    sums = pltpu.roll(sums, HD, 1)
    return (context / sums).astype(jnp.bfloat16)


def inner_kernel(numbers, q_ref, kv_ref, out_ref):
    half_len, quarter = SPAN // 2, SPAN // 4
    width = q_ref.shape[1]

    @pl.loop(0, width // LANES)
    def _(pair):
        lanes = pl.ds(pl.multiple_of(pair * LANES, LANES), LANES)
        v_lanes = pl.ds(pl.multiple_of(pair * LANES + width, LANES), LANES)
        for place, number in enumerate(numbers):
            start = number * half_len
            keys = slice(start - quarter, start - quarter + SPAN)
            out_ref[place * half_len : (place + 1) * half_len, lanes] = attend_pair(
                q_ref[start : start + half_len, lanes], kv_ref[keys, lanes], kv_ref[keys, v_lanes], None, None
            )


def put_rows(out_ref, start, lanes, value, tp_count):
    if out_ref.ndim == 2:
        out_ref[start : start + value.shape[0], lanes] = value
        return
    stripe = out_ref.shape[1]
    seq_count = out_ref.shape[0] // tp_count
    row, end = start, start + value.shape[0]
    while row < end:
        number, within = divmod(row, stripe)
        part, place = divmod(number, seq_count)
        upto = min(end, (number + 1) * stripe)
        out_ref[place * tp_count + part, within : within + upto - row, lanes] = value[row - start : upto - start]
        row = upto


def outer_kernel(tp_count, edge_ref, q_ref, kv_ref, low_ref, high_ref, inner_ref, out_ref):
    half_len, quarter = SPAN // 2, SPAN // 4
    rows, width = q_ref.shape
    inside = SPAN - quarter

    @pl.loop(0, width // LANES)
    def _(pair):
        lanes = pl.ds(pl.multiple_of(pair * LANES, LANES), LANES)
        v_lanes = pl.ds(pl.multiple_of(pair * LANES + width, LANES), LANES)
        put_rows(out_ref, half_len, lanes, inner_ref[:, lanes], tp_count)
        key = jnp.concatenate([low_ref[:, lanes], kv_ref[:inside, lanes]], axis=0)
        value = jnp.concatenate([low_ref[:, v_lanes], kv_ref[:inside, v_lanes]], axis=0)
        first = attend_pair(q_ref[:half_len, lanes], key, value, edge_ref[0] != 0, None)
        put_rows(out_ref, 0, lanes, first, tp_count)
        key = jnp.concatenate([kv_ref[rows - inside :, lanes], high_ref[:, lanes]], axis=0)
        value = jnp.concatenate([kv_ref[rows - inside :, v_lanes], high_ref[:, v_lanes]], axis=0)
        last = attend_pair(q_ref[rows - half_len :, lanes], key, value, None, edge_ref[1] != 0)
        put_rows(out_ref, rows - half_len, lanes, last, tp_count)


def attention_cost(blocks, width):
    half_len = SPAN // 2
    return pl.CostEstimate(
        flops=8 * blocks * half_len * SPAN * width,
        bytes_accessed=2 * blocks * (2 * half_len + 2 * SPAN) * width,
        transcendentals=blocks * half_len * SPAN * width // HD,
    )


def attend_inner(queries, both):
    half_len = SPAN // 2
    rows, width = queries.shape
    numbers = tuple(range(1, rows // half_len - 1))
    return pl.pallas_call(
        functools.partial(inner_kernel, numbers),
        in_specs=[VMEM] * 2,
        out_specs=VMEM,
        out_shape=jax.ShapeDtypeStruct((len(numbers) * half_len, width), jnp.bfloat16),
        cost_estimate=attention_cost(len(numbers), width),
        compiler_params=pltpu.CompilerParams(vmem_limit_bytes=GRANT),
        name="inner_blocks",
    )(queries, both)


def attend_outer(queries, both, low, high, inner, at_start, at_end, seq_count, tp_count):
    rows, width = queries.shape
    stripe = rows // (seq_count * tp_count)
    in_place = stripe % 8 == 0
    shape = (seq_count * tp_count, stripe, width) if in_place else (rows, width)
    edges = jnp.stack([at_start, at_end]).astype(jnp.int32)
    context = pl.pallas_call(
        functools.partial(outer_kernel, tp_count),
        in_specs=[SMEM] + [VMEM] * 5,
        out_specs=VMEM,
        out_shape=jax.ShapeDtypeStruct(shape, jnp.bfloat16),
        cost_estimate=attention_cost(2, width),
        compiler_params=pltpu.CompilerParams(vmem_limit_bytes=GRANT),
        name="outer_blocks",
    )(edges, queries, both, low, high, inner)
    if not in_place:
        context = context.reshape(tp_count, seq_count, stripe, width).transpose(1, 0, 2, 3)
    return context.reshape(seq_count * tp_count, stripe, width)


def project_kernel(sources, slots, place_ref, order_ref, got_ref, hidden_ref, own_ref, *refs):
    parts, out_ref, (context_ref, held_ref, sems) = refs[:-4], refs[-4], refs[-3:]
    depth = own_ref.shape[0]
    tp_count = order_ref.shape[0]
    part_depth, columns = parts[0].shape[1:]

    def block(e):
        return pl.ds(pl.multiple_of(place_ref[e] * columns, LANES), columns)

    def copies(e):
        slot = e % slots
        yield pltpu.make_async_copy(own_ref.at[:, block(e)], held_ref.at[slot, :depth], sems.at[slot, 0])
        for n, (i, j) in enumerate(sources[e]):
            rows = slice(depth + n * part_depth, depth + (n + 1) * part_depth)
            yield pltpu.make_async_copy(parts[i].at[j], held_ref.at[slot, rows], sems.at[slot, n + 1])

    for e in range(min(slots, len(sources))):
        for copy in copies(e):
            copy.start()
    if got_ref.ndim == 3:
        stripe = got_ref.shape[1]
        for k in range(tp_count):
            for a in range(got_ref.shape[0] // tp_count):
                context_ref[a * stripe : (a + 1) * stripe, k * depth : (k + 1) * depth] = got_ref[
                    a * tp_count + order_ref[k]
                ]
    else:
        for k in range(tp_count):
            lanes = pl.ds(pl.multiple_of(order_ref[k] * depth, LANES), depth)
            context_ref[:, k * depth : (k + 1) * depth] = got_ref[:, lanes]
    for e in range(len(sources)):
        for copy in copies(e):
            copy.wait()
        total = jnp.dot(context_ref[...], held_ref[e % slots], preferred_element_type=jnp.float32)
        out_ref[:, block(e)] = (hidden_ref[:, block(e)].astype(jnp.float32) + total).astype(out_ref.dtype)
        if e + slots < len(sources):
            for copy in copies(e + slots):
                copy.start()


def project(places, order, sources, got, hidden, own, parts):
    rows, width = hidden.shape
    if got.shape[1] % 8:
        tp_count = order.shape[0]
        got = got.reshape(-1, tp_count, *got.shape[1:]).transpose(0, 2, 1, 3).reshape(rows, -1)
    depth = own.shape[0] * order.shape[0]
    columns = parts[0].shape[2]
    slots = 3
    return pl.pallas_call(
        functools.partial(project_kernel, sources, slots),
        in_specs=[SMEM] * 2 + [VMEM] * 2 + [ANY] * (1 + len(parts)),
        out_specs=VMEM,
        out_shape=jax.ShapeDtypeStruct(hidden.shape, jnp.bfloat16),
        scratch_shapes=[
            pltpu.VMEM((rows, depth), jnp.bfloat16),
            pltpu.VMEM((slots, depth, columns), jnp.bfloat16),
            pltpu.SemaphoreType.DMA((slots, 1 + len(sources[0]))),
        ],
        cost_estimate=pl.CostEstimate(
            flops=2 * rows * depth * width, bytes_accessed=2 * depth * width, transcendentals=0
        ),
        name="project",
    )(places, order, got, hidden, own, *parts)


def share_orders(seq_count):
    bits = [1 << i for i in range(seq_count.bit_length() - 1)]
    outer = bits[1:]
    return [outer + bits[:1], outer[::-1] + bits[:1]]


def share(piece, order, seq_count):
    levels = [piece[None]]
    for bit in order:
        pairs = [(i, i ^ bit) for i in range(seq_count)]
        held = jnp.concatenate(levels, axis=0) if len(levels) > 1 else levels[0]
        levels.append(lax.ppermute(held, "seq", pairs))
    return levels


def offsets(order):
    held = [0]
    for bit in order:
        held = held + [offset ^ bit for offset in held]
    return held


def level_of(entry):
    level = entry.bit_length()
    return level, entry - (1 << level >> 1)


def offsets(order):
    held = [0]
    for bit in order:
        held = held + [offset ^ bit for offset in held]
    return held


def on_device(hidden_in, norm_gain, w_qkv, w_out):
    seq_count, tp_count = lax.axis_size("seq"), lax.axis_size("tp")
    seq_index, tp_index = lax.axis_index("seq"), lax.axis_index("tp")
    own_rows, model_width = hidden_in.shape
    width = w_qkv.shape[2]
    quarter = SPAN // 4
    stripe = own_rows // seq_count
    rows = own_rows * tp_count
    columns = model_width // seq_count
    ring = [(i, (i + 1) % tp_count) for i in range(tp_count)]

    pieces_of_w = [lax.dynamic_slice_in_dim(w_out, seq_index * columns, columns, 1)]
    first_piece, hidden_in = lax.optimization_barrier((pieces_of_w[0], hidden_in))
    pieces_of_w.append(lax.ppermute(first_piece, "tp", ring))
    orders = share_orders(seq_count)

    chunk = own_rows // CHUNKS
    pieces = [rms_scale(hidden_in, norm_gain, i * chunk, chunk) for i in range(CHUNKS)]
    queries = jnp.zeros((rows, width), jnp.bfloat16)
    both = jnp.zeros((rows, 2 * width), jnp.bfloat16)
    hidden = None
    for step in range(tp_count):
        last = step == tp_count - 1
        following = []
        if not last:
            for piece in pieces:
                following.append(lax.ppermute(piece, "tp", ring))
        elif len(pieces_of_w) < tp_count:
            held, pieces[-1] = lax.optimization_barrier((pieces_of_w[-1], pieces[-1]))
            pieces_of_w.append(lax.ppermute(held, "tp", ring))
        start = lax.rem(tp_index - step + tp_count, tp_count) * own_rows
        for i, piece in enumerate(pieces):
            products = []
            for which in range(3):
                product = jnp.dot(piece, w_qkv[which], preferred_element_type=jnp.float32)
                products.append(product.astype(jnp.bfloat16))
            at = start + i * chunk
            both = lax.dynamic_update_slice(both, products[1], (at, jnp.int32(0)))
            both = lax.dynamic_update_slice(both, products[2], (at, jnp.int32(width)))
            queries = lax.dynamic_update_slice(queries, products[0], (at, jnp.int32(0)))
        pieces = following
        if step == 0:
            hidden = lax.all_to_all(
                hidden_in.reshape(seq_count, stripe, model_width), "seq", split_axis=0, concat_axis=0, tiled=True
            ).reshape(own_rows, model_width)
        if step == 1:
            hidden, queries = lax.optimization_barrier((hidden, queries))
        if not last and step + 1 < EARLY:
            held, pieces = lax.optimization_barrier((pieces_of_w[-1], pieces))
            pieces_of_w.append(lax.ppermute(held, "tp", ring))

    forward = [(i, i + 1) for i in range(seq_count - 1)]
    backward = [(i + 1, i) for i in range(seq_count - 1)]
    low = lax.ppermute(both[rows - quarter :], "seq", forward)
    high = lax.ppermute(both[:quarter], "seq", backward)
    inner = attend_inner(queries, both)
    while len(pieces_of_w) < tp_count:
        pieces_of_w.append(lax.ppermute(pieces_of_w[-1], "tp", ring))
    sent = attend_outer(
        queries, both, low, high, inner, seq_index == 0, seq_index == seq_count - 1, seq_count, tp_count
    )
    got = lax.all_to_all(sent, ("seq", "tp"), split_axis=0, concat_axis=0, tiled=True)

    levels = []
    for k, piece in enumerate(pieces_of_w[1:], 1):
        half = piece.shape[0] // 2
        levels.append([share(piece[h * half : (h + 1) * half], orders[h], seq_count) for h in range(2)])
    places, sources = [], []
    parts = [part for halves in levels for half in halves for part in half]
    per = len(levels[0][0])
    found = [offsets(order) for order in orders]
    for offset in range(seq_count):
        places.append(offset)
        source = []
        for k in range(len(levels)):
            for h in range(2):
                level, entry = level_of(found[h].index(offset))
                source.append(((2 * k + h) * per + level, entry))
        sources.append(tuple(source))
    places = seq_index ^ jnp.array(places, jnp.int32)
    order = lax.rem(tp_index - jnp.arange(tp_count, dtype=jnp.int32) + tp_count, tp_count)
    return project(places, order, tuple(sources), got, hidden, w_out, parts)


def solution(mesh):
    return jax.shard_map(
        on_device,
        mesh=mesh,
        in_specs=(P(("seq", "tp"), None), P(), P(None, None, "tp"), P("tp", None)),
        out_specs=P(("seq", "tp"), None),
        check_vma=False,
    )
```
